256 devices in a mesh: ka: 8 (over y_lo, x), pw: 32 (over y_hi, z, core).
Axes of the slice: x: 4, y: 4 (y_hi: 2, y_lo: 2; y = y_hi * 2 + y_lo), z: 8, core: 2. Of those that a mesh axis runs over, the one named last changes fastest.
Arguments:
- states_re: bfloat16 [16, 512, 32768], P('ka', None, 'pw'), may hold values from -0.016572815 to 0.016572815
- states_im: bfloat16 [16, 512, 32768], P('ka', None, 'pw'), may hold values from -0.016572815 to 0.016572815
Outputs:
- wilson_lines: float32 [16, 512, 2, 512], P('ka', 'pw')
The draws below stay inside these ranges and needn't reach their ends.
All inputs are finite; a program needn't handle non-finite values.
Results may differ from the reference program's by a relative error of at most 0.0003.
Values may be sent and summed in bfloat16 or wider, within the bound.
A program may use at most 64 MiB of HBM per device.

```python
import math
import jax
import jax.numpy as jnp
from jax import lax

NB = 512
NPW = 32768
NK = 16


def state_parts(key):
    freqs = jax.random.permutation(jax.random.fold_in(key, 6), NPW)[:NB].astype(jnp.int32)
    waves = jnp.arange(NPW, dtype=jnp.int32)
    turns = freqs[:, None] * waves[None, :] % NPW
    phases = jax.random.uniform(jax.random.fold_in(key, 5), (NK, NB, 1), jnp.float32, -math.pi, math.pi)
    angle = 2.0 * math.pi / NPW * turns.astype(jnp.float32)[None, :, :] + phases
    noise_re = jnp.clip(jax.random.normal(jax.random.fold_in(key, 7), (NK, NB, NPW), jnp.float32), -4.0, 4.0)
    noise_im = jnp.clip(jax.random.normal(jax.random.fold_in(key, 8), (NK, NB, NPW), jnp.float32), -4.0, 4.0)
    noise_scale = 0.6 / math.sqrt(2.0 * NPW)
    base_scale = 1.0 / math.sqrt(NPW)
    return (base_scale * jnp.cos(angle) + noise_scale * noise_re, base_scale * jnp.sin(angle) + noise_scale * noise_im)


def draw_states_re(key, part):
    return state_parts(key)[0].astype(jnp.bfloat16)


def draw_states_im(key, part):
    return state_parts(key)[1].astype(jnp.bfloat16)


def setup_inputs(seed: int = 0) -> dict:
    arg_keys = jax.random.split(jax.random.key(seed), 3)
    states_re = draw_states_re(jax.random.fold_in(arg_keys[2], 71), 0)
    states_im = draw_states_im(jax.random.fold_in(arg_keys[2], 71), 0)
    return dict(states_re=states_re, states_im=states_im)


def complex_rows(left, right):
    highest = lax.Precision.HIGHEST
    left_re = left[:, 0]
    left_im = left[:, 1]
    right_re = right[:, 0]
    right_im = right[:, 1]
    real_part = jnp.dot(left_re, right_re, precision=highest, preferred_element_type=jnp.float32) - jnp.dot(left_im, right_im, precision=highest, preferred_element_type=jnp.float32)
    imag_part = jnp.dot(left_re, right_im, precision=highest, preferred_element_type=jnp.float32) + jnp.dot(left_im, right_re, precision=highest, preferred_element_type=jnp.float32)
    return jnp.stack([real_part, imag_part], 1)


def reference(states_re, states_im):
    highest = lax.Precision.HIGHEST

    def margin_at(kpoint):
        later = (kpoint + 1) % NK
        own_re = states_re[kpoint].astype(jnp.float32)
        own_im = states_im[kpoint].astype(jnp.float32)
        next_re = states_re[later].astype(jnp.float32)
        next_im = states_im[later].astype(jnp.float32)
        real_part = jnp.dot(own_re, next_re.T, precision=highest, preferred_element_type=jnp.float32) + jnp.dot(own_im, next_im.T, precision=highest, preferred_element_type=jnp.float32)
        imag_part = jnp.dot(own_re, next_im.T, precision=highest, preferred_element_type=jnp.float32) - jnp.dot(own_im, next_re.T, precision=highest, preferred_element_type=jnp.float32)
        return jnp.stack([real_part, imag_part], 1)

    margins = lax.map(margin_at, jnp.arange(NK, dtype=jnp.int32))
    identity = jnp.stack([jnp.eye(NB, dtype=jnp.float32), jnp.zeros((NB, NB), jnp.float32)], 1)

    def advance(carry, margin):
        line = complex_rows(carry, margin)
        return line, line

    final_line, lines = lax.scan(advance, identity, margins)
    return lines
```

```python
import functools
import heapq

import jax
import jax.numpy as jnp
from jax import lax
from jax.experimental import pallas as pl
from jax.experimental.pallas import tpu as pltpu
from jax.sharding import PartitionSpec as P

F32 = jnp.float32
BF16 = jnp.bfloat16
WIDTH = 128
SEMS = 256


def high_low(value):
    high = value.astype(BF16)
    return high, (value - high.astype(F32)).astype(BF16)


def dot(left, right):
    return jnp.dot(left, right, preferred_element_type=F32)


def dot_t(left, right):
    return lax.dot_general(left, right, (((1,), (1,)), ((), ())), preferred_element_type=F32)


def kernel(
    ka_size, zsize,
    re_hbm, im_hbm, out_ref,
    st_re, st_im, halo_re, halo_im, part, core_in, plus_in, minus_in, y_in, full,
    lhs0, m0_high, m0_low, p_high, p_low, rows_in, rows_out, stack,
    load_sem, send_sem, recv_sem,
):
    bands = st_re.shape[1]
    chunks = bands // WIDTH
    wide = 2 * WIDTH
    half = bands // 2
    piece = half // zsize
    small = piece // 2
    reach = zsize // 2
    own = rows_in.shape[0]

    ka = lax.axis_index("ka")
    pw = lax.axis_index("pw")
    core = lax.rem(pw, 2)
    z = lax.rem(pw // 2, zsize)
    yhi = pw // (2 * zsize)

    def pw_of(y, zz, c):
        return (y * zsize + zz) * 2 + c

    def up(n):
        return lax.rem(z + n, zsize)

    def down(n):
        return lax.rem(z + zsize - n, zsize)

    to_core = {"ka": ka, "pw": pw_of(yhi, z, 1 - core)}
    to_up = {"ka": ka, "pw": pw_of(yhi, up(1), core)}
    to_down = {"ka": ka, "pw": pw_of(yhi, down(1), core)}
    to_y = {"ka": ka, "pw": pw_of(1 - yhi, z, core)}
    to_next = {"ka": lax.rem(ka + 1, ka_size), "pw": pw}
    to_prev = {"ka": lax.rem(ka + ka_size - 1, ka_size), "pw": pw}

    loads = [
        pltpu.make_async_copy(re_hbm, st_re, load_sem.at[0]),
        pltpu.make_async_copy(im_hbm, st_im, load_sem.at[1]),
    ]
    for load in loads:
        load.start()

    barrier = pltpu.get_barrier_semaphore()
    partners = (to_core, to_up, to_down, to_y, to_next, to_prev)
    for partner in partners:
        pl.semaphore_signal(barrier, inc=1, device_id=partner, device_id_type=pl.DeviceIdType.MESH)
    pl.semaphore_wait(barrier, len(partners))

    started = []

    def copy(src, dst, device, start=True):
        n = len(started)
        made = pltpu.make_async_remote_copy(
            src_ref=src, dst_ref=dst, send_sem=send_sem.at[n], recv_sem=recv_sem.at[n],
            device_id=device, device_id_type=pl.DeviceIdType.MESH,
        )
        started.append(made)
        if start:
            made.start()
        return made

    halo = []
    for chunk in range(chunks):
        rows = pl.ds(chunk * WIDTH, WIDTH)
        halo.append((
            copy(re_hbm.at[0, rows], halo_re.at[rows], to_prev),
            copy(im_hbm.at[0, rows], halo_im.at[rows], to_prev),
        ))
    for load in loads:
        load.wait()

    def rows_of(zz, c, offset=0, count=None):
        count = piece if count is None else count
        start = c * half + zz * piece + offset
        return pl.ds(pl.multiple_of(start, small), count)

    def partial_sum(k, chunk, slot):
        columns = pl.ds(chunk * WIDTH, WIDTH)
        if k == 0:
            right_re, right_im = st_re[1, columns], st_im[1, columns]
        else:
            right_re, right_im = halo_re[columns], halo_im[columns]
        tile = min(bands, 256)

        @pl.loop(0, bands // tile)
        def _(step):
            rows = pl.ds(pl.multiple_of(step * tile, tile), tile)
            left_re, left_im = st_re[k, rows], st_im[k, rows]
            part[slot, rows, :WIDTH] = dot_t(left_re, right_re) + dot_t(left_im, right_im)
            part[slot, rows, WIDTH:] = dot_t(left_re, right_im) - dot_t(left_im, right_re)

    def finish_first(chunk, slot):
        columns = pl.ds(chunk * WIDTH, WIDTH)
        both = pl.ds(chunk * wide, wide)
        high, low = high_low(full[slot])
        m0_high[:, both] = high
        m0_low[:, both] = low
        lhs0[0, :, columns] = high[:, :WIDTH]
        lhs0[1, :, columns] = low[:, :WIDTH]
        lhs0[2, :, columns] = high[:, WIDTH:]
        lhs0[3, :, columns] = low[:, WIDTH:]

    def finish_second(chunk, slot):
        both = pl.ds(chunk * wide, wide)
        high, low = high_low(full[slot])
        tile = min(bands, 128)

        @pl.loop(0, bands // tile)
        def _(step):
            rows = pl.ds(pl.multiple_of(step * tile, tile), tile)
            re_high, re_low = lhs0[0, rows], lhs0[1, rows]
            im_high, im_low = lhs0[2, rows], lhs0[3, rows]
            by_re = dot(re_high, high) + (dot(re_low, high) + dot(re_high, low))
            by_im = dot(im_high, high) + (dot(im_low, high) + dot(im_high, low))
            new_re = by_re[:, :WIDTH] - by_im[:, WIDTH:]
            new_im = by_re[:, WIDTH:] + by_im[:, :WIDTH]
            span_high, span_low = high_low(jnp.concatenate([new_re, new_im], 1))
            p_high[rows, both] = span_high
            p_low[rows, both] = span_low

    def margin_chunk(k, chunk):
        slot = k * chunks + chunk
        if k == 1:
            halo[chunk][0].wait_recv()
            halo[chunk][1].wait_recv()
        partial_sum(k, chunk, slot)
        mine = pl.ds(pl.multiple_of(core * half, half), half)
        theirs = pl.ds(pl.multiple_of((1 - core) * half, half), half)
        crossing = copy(part.at[slot, theirs], core_in.at[slot], to_core)
        yield 1.6
        crossing.wait_recv()
        part[slot, mine] = part[slot, mine] + core_in[slot]
        far = up(reach)
        going_up = copy(
            part.at[slot, rows_of(far, core, 0, small)], plus_in.at[slot, 0, pl.ds(0, small)], to_up
        )
        going_down = copy(
            part.at[slot, rows_of(far, core, small, small)], minus_in.at[slot, 0, pl.ds(small, small)], to_down
        )
        yield 2.2
        for step in range(1, reach):
            going_up.wait_recv()
            going_down.wait_recv()
            there_up, there_down = up(reach - step), down(reach - step)
            if step == 1:
                at_up, at_down = rows_of(there_up, core, 0, small), rows_of(there_down, core, small, small)
                got_up, got_down = plus_in[slot, 0, :small], minus_in[slot, 0, small:]
            else:
                at_up, at_down = rows_of(there_up, core), rows_of(there_down, core)
                got_up, got_down = plus_in[slot, step - 1], minus_in[slot, step - 1]
            part[slot, at_up] = part[slot, at_up] + got_up
            part[slot, at_down] = part[slot, at_down] + got_down
            going_up = copy(part.at[slot, rows_of(there_up, core)], plus_in.at[slot, step], to_up)
            going_down = copy(part.at[slot, rows_of(there_down, core)], minus_in.at[slot, step], to_down)
            yield 2.5
        going_up.wait_recv()
        going_down.wait_recv()
        here = rows_of(z, core)
        if reach == 1:
            low_rows, high_rows = rows_of(z, core, 0, small), rows_of(z, core, small, small)
            part[slot, low_rows] = part[slot, low_rows] + plus_in[slot, 0, :small]
            part[slot, high_rows] = part[slot, high_rows] + minus_in[slot, 0, small:]
        else:
            part[slot, here] = part[slot, here] + plus_in[slot, reach - 1] + minus_in[slot, reach - 1]
        crossing = copy(part.at[slot, here], y_in.at[slot], to_y)
        yield 3.0
        crossing.wait_recv()
        full[slot, here] = part[slot, here] + y_in[slot]
        from_core = []

        def across(zz, offset=0, count=None):
            mine = full.at[slot, rows_of(zz, core, offset, count)]
            from_core.append(copy(mine, mine, to_core))

        def along(zz, device, offset=0, count=None):
            mine = full.at[slot, rows_of(zz, core, offset, count)]
            return copy(mine, mine, device)

        for step in range(reach):
            if step:
                going_up.wait_recv()
                going_down.wait_recv()
            last = step == reach - 1
            if last:
                going_up = along(down(step), to_up, 0, small)
                going_down = along(up(step), to_down, small, small)
            else:
                going_up = along(down(step), to_up)
                going_down = along(up(step), to_down)
            across(down(step))
            if step:
                across(up(step))
            yield 2.5
        going_up.wait_recv()
        going_down.wait_recv()
        across(down(reach))
        yield 1.2
        for crossing in from_core:
            crossing.wait_recv()
        if k == 0:
            finish_first(chunk, slot)
        else:
            finish_second(chunk, slot)

    order = []
    for chunk in range(chunks):
        order.append((1.0 + 0.7 * chunk, len(order), margin_chunk(0, chunk)))
    for chunk in range(chunks):
        order.append((11.5 * (chunk + 1), len(order), margin_chunk(1, chunk)))
    heapq.heapify(order)
    while order:
        when, n, steps = heapq.heappop(order)
        wait = next(steps, None)
        if wait is not None:
            heapq.heappush(order, (when + wait, n, steps))

    def apply(high_ref, low_ref):
        left = stack[...]
        short = jnp.concatenate([left[:own], left[2 * own:3 * own]], 0)
        pieces_re, pieces_im = [], []
        for chunk in range(chunks):
            both = pl.ds(chunk * wide, wide)
            with_high = dot(left, high_ref[:, both])
            with_low = dot(short, low_ref[:, both])
            by_re = with_high[:own] + (with_high[own:2 * own] + with_low[:own])
            by_im = with_high[2 * own:3 * own] + (with_high[3 * own:] + with_low[own:])
            pieces_re.append(by_re[:, :WIDTH] - by_im[:, WIDTH:])
            pieces_im.append(by_re[:, WIDTH:] + by_im[:, :WIDTH])
        return jnp.concatenate(pieces_re, 1), jnp.concatenate(pieces_im, 1)

    handed = copy(rows_out, rows_in, to_next, start=False)

    @pl.when(ka == 0)
    def _():
        row = lax.broadcasted_iota(jnp.int32, (own, 2 * bands), 0) + pw * own
        column = lax.broadcasted_iota(jnp.int32, (own, 2 * bands), 1)
        one = (row == column).astype(F32)
        high, low = high_low(one)
        stack[...] = jnp.concatenate([high[:, :bands], low[:, :bands], high[:, bands:], low[:, bands:]], 0)

    @pl.when(ka > 0)
    def _():
        handed.wait_recv()
        high, low = high_low(rows_in[...])
        stack[...] = jnp.concatenate([high[:, :bands], low[:, :bands], high[:, bands:], low[:, bands:]], 0)

    line_re, line_im = apply(p_high, p_low)
    rows_out[:, :bands] = line_re
    rows_out[:, bands:] = line_im

    @pl.when(ka < ka_size - 1)
    def _():
        handed.start()

    out_ref[1, 0] = line_re
    out_ref[1, 1] = line_im
    line_re, line_im = apply(m0_high, m0_low)
    out_ref[0, 0] = line_re
    out_ref[0, 1] = line_im

    for made in started[:-1]:
        made.wait_send()

    @pl.when(ka < ka_size - 1)
    def _():
        handed.wait_send()


def shards(ka_size, pw_size, states_re, states_im):
    _, bands, waves = states_re.shape
    zsize = pw_size // 4
    own = bands // pw_size
    chunks = bands // WIDTH
    slots = 2 * chunks
    wide = 2 * WIDTH
    half = bands // 2
    piece = half // zsize
    reach = zsize // 2
    any_space = pl.BlockSpec(memory_space=pl.ANY)
    lines = pl.pallas_call(
        functools.partial(kernel, ka_size, zsize),
        out_shape=jax.ShapeDtypeStruct((2, 2, own, bands), F32),
        in_specs=[any_space, any_space],
        out_specs=pl.BlockSpec(memory_space=pltpu.VMEM),
        scratch_shapes=[
            pltpu.VMEM((2, bands, waves), BF16),
            pltpu.VMEM((2, bands, waves), BF16),
            pltpu.VMEM((bands, waves), BF16),
            pltpu.VMEM((bands, waves), BF16),
            pltpu.VMEM((slots, bands, wide), F32),
            pltpu.VMEM((slots, half, wide), F32),
            pltpu.VMEM((slots, reach, piece, wide), F32),
            pltpu.VMEM((slots, reach, piece, wide), F32),
            pltpu.VMEM((slots, piece, wide), F32),
            pltpu.VMEM((slots, bands, wide), F32),
            pltpu.VMEM((4, bands, bands), BF16),
            pltpu.VMEM((bands, 2 * bands), BF16),
            pltpu.VMEM((bands, 2 * bands), BF16),
            pltpu.VMEM((bands, 2 * bands), BF16),
            pltpu.VMEM((bands, 2 * bands), BF16),
            pltpu.VMEM((own, 2 * bands), F32),
            pltpu.VMEM((own, 2 * bands), F32),
            pltpu.VMEM((4 * own, bands), BF16),
            pltpu.SemaphoreType.DMA((2,)),
            pltpu.SemaphoreType.DMA((SEMS,)),
            pltpu.SemaphoreType.DMA((SEMS,)),
        ],
        compiler_params=pltpu.CompilerParams(
            collective_id=0, has_side_effects=True, vmem_limit_bytes=56 * 1024 * 1024
        ),
    )(states_re, states_im)
    return jnp.transpose(lines, (0, 2, 1, 3))


def solution(mesh):
    in_specs = (P("ka", None, "pw"), P("ka", None, "pw"))
    out_specs = P("ka", "pw", None, None)
    body = functools.partial(shards, mesh.shape["ka"], mesh.shape["pw"])
    return jax.shard_map(body, mesh=mesh, in_specs=in_specs, out_specs=out_specs, check_vma=False)
```

```python
import functools
import heapq

import jax
import jax.numpy as jnp
from jax import lax
from jax.experimental import pallas as pl
from jax.experimental.pallas import tpu as pltpu
from jax.sharding import PartitionSpec as P

F32 = jnp.float32
BF16 = jnp.bfloat16
WIDTH = 128
SEMS = 256


def high_low(value):
    high = value.astype(BF16)
    return high, (value - high.astype(F32)).astype(BF16)


def dot(left, right):
    return jnp.dot(left, right, preferred_element_type=F32)


def dot_t(left, right):
    return lax.dot_general(left, right, (((1,), (1,)), ((), ())), preferred_element_type=F32)


def kernel(
    ka_size, zsize,
    re_hbm, im_hbm, out_ref,
    st_re, st_im, part, core_in, plus_in, minus_in, y_in, mix_in, full,
    lhs0, m0_high, m0_low, p_high, p_low, rows_in, rows_out, stack,
    load_sem, send_sem, recv_sem,
):
    bands = st_re.shape[1]
    chunks = bands // WIDTH
    wide = 2 * WIDTH
    half = bands // 2
    piece = half // zsize
    reach = zsize // 2
    own = rows_in.shape[0]

    ka = lax.axis_index("ka")
    pw = lax.axis_index("pw")
    core = lax.rem(pw, 2)
    z = lax.rem(pw // 2, zsize)
    yhi = pw // (2 * zsize)

    def device(k, y, zz, c):
        return {"ka": lax.rem(k + ka_size, ka_size), "pw": (y * zsize + zz) * 2 + c}

    def up(n):
        return lax.rem(z + n, zsize)

    def down(n):
        return lax.rem(z + zsize - n, zsize)

    to_core = device(ka, yhi, z, 1 - core)
    to_up = device(ka, yhi, up(1), core)
    to_down = device(ka, yhi, down(1), core)
    to_y = device(ka, 1 - yhi, z, core)
    to_next = device(ka + 1, yhi, z, core)
    to_prev = device(ka - 1, yhi, z, core)
    to_halo = device(ka - 1 + 2 * core, yhi, z, core)
    from_halo = device(ka + 1 - 2 * core, yhi, z, core)
    to_mix = (
        device(ka - core, yhi, z, 1 - core),
        device(ka - core, 1 - yhi, z, core),
        device(ka - core, 1 - yhi, z, 1 - core),
        to_prev,
    )
    from_mix = (
        device(ka + 1 - core, yhi, z, 1 - core),
        device(ka + core, 1 - yhi, z, core),
        device(ka + 1 - core, 1 - yhi, z, 1 - core),
        to_next,
    )

    loads = [
        pltpu.make_async_copy(re_hbm, st_re.at[pl.ds(0, 2)], load_sem.at[0]),
        pltpu.make_async_copy(im_hbm, st_im.at[pl.ds(0, 2)], load_sem.at[1]),
    ]
    for load in loads:
        load.start()

    barrier = pltpu.get_barrier_semaphore()
    senders = (to_core, to_up, to_down, to_y, to_prev, from_halo) + from_mix
    for sender in senders:
        pl.semaphore_signal(barrier, inc=1, device_id=sender, device_id_type=pl.DeviceIdType.MESH)
    pl.semaphore_wait(barrier, len(senders))

    started = []
    numbered = [0]

    def prepare(src, dst, target):
        n = numbered[0]
        numbered[0] += 1
        return pltpu.make_async_remote_copy(
            src_ref=src, dst_ref=dst, send_sem=send_sem.at[n], recv_sem=recv_sem.at[n],
            device_id=target, device_id_type=pl.DeviceIdType.MESH,
        )

    def copy(src, dst, target):
        made = prepare(src, dst, target)
        made.start()
        started.append(made)
        return made

    halo = (copy(re_hbm.at[core], st_re.at[2], to_halo), copy(im_hbm.at[core], st_im.at[2], to_halo))
    for load in loads:
        load.wait()

    def partial_sum(left, right, chunk, slot):
        columns = pl.ds(chunk * WIDTH, WIDTH)
        right_re, right_im = st_re[right, columns], st_im[right, columns]
        tile = min(bands, 256)

        @pl.loop(0, bands // tile)
        def _(step):
            rows = pl.ds(pl.multiple_of(step * tile, tile), tile)
            left_re, left_im = st_re[left, rows], st_im[left, rows]
            part[slot, rows, :WIDTH] = dot_t(left_re, right_re) + dot_t(left_im, right_im)
            part[slot, rows, WIDTH:] = dot_t(left_re, right_im) - dot_t(left_im, right_re)

    def finish_first(chunk, slot):
        columns = pl.ds(chunk * WIDTH, WIDTH)
        both = pl.ds(chunk * wide, wide)
        high, low = high_low(full[slot])
        m0_high[:, both] = high
        m0_low[:, both] = low
        lhs0[0, :, columns] = high[:, :WIDTH]
        lhs0[1, :, columns] = low[:, :WIDTH]
        lhs0[2, :, columns] = high[:, WIDTH:]
        lhs0[3, :, columns] = low[:, WIDTH:]

    def finish_second(chunk, slot):
        both = pl.ds(chunk * wide, wide)
        high, low = high_low(full[slot])
        tile = min(bands, 128)

        @pl.loop(0, bands // tile)
        def _(step):
            rows = pl.ds(pl.multiple_of(step * tile, tile), tile)
            re_high, re_low = lhs0[0, rows], lhs0[1, rows]
            im_high, im_low = lhs0[2, rows], lhs0[3, rows]
            by_re = dot(re_high, high) + (dot(re_low, high) + dot(re_high, low))
            by_im = dot(im_high, high) + (dot(im_low, high) + dot(im_high, low))
            new_re = by_re[:, :WIDTH] - by_im[:, WIDTH:]
            new_im = by_re[:, WIDTH:] + by_im[:, :WIDTH]
            span_high, span_low = high_low(jnp.concatenate([new_re, new_im], 1))
            p_high[rows, both] = span_high
            p_low[rows, both] = span_low

    def scatter(slot, base, size, pace):
        small = size // 2

        def rows(zz, offset=0, count=size):
            return pl.ds(pl.multiple_of(base + zz * size + offset, 8), count)

        far = up(reach)
        going_up = copy(
            part.at[slot, rows(far, 0, small)], plus_in.at[slot, 0, pl.ds(0, small)], to_up
        )
        going_down = copy(
            part.at[slot, rows(far, small, small)], minus_in.at[slot, 0, pl.ds(small, small)], to_down
        )
        yield pace
        for step in range(1, reach):
            going_up.wait_recv()
            going_down.wait_recv()
            there_up, there_down = up(reach - step), down(reach - step)
            if step == 1:
                at_up, at_down = rows(there_up, 0, small), rows(there_down, small, small)
                got_up, got_down = plus_in[slot, 0, :small], minus_in[slot, 0, small:size]
            else:
                at_up, at_down = rows(there_up), rows(there_down)
                got_up, got_down = plus_in[slot, step - 1, :size], minus_in[slot, step - 1, :size]
            part[slot, at_up] = part[slot, at_up] + got_up
            part[slot, at_down] = part[slot, at_down] + got_down
            going_up = copy(part.at[slot, rows(there_up)], plus_in.at[slot, step, pl.ds(0, size)], to_up)
            going_down = copy(part.at[slot, rows(there_down)], minus_in.at[slot, step, pl.ds(0, size)], to_down)
            yield pace
        going_up.wait_recv()
        going_down.wait_recv()
        if reach == 1:
            first, second = rows(z, 0, small), rows(z, small, small)
            part[slot, first] = part[slot, first] + plus_in[slot, 0, :small]
            part[slot, second] = part[slot, second] + minus_in[slot, 0, small:size]
        else:
            here = rows(z)
            part[slot, here] = part[slot, here] + plus_in[slot, reach - 1, :size] + minus_in[slot, reach - 1, :size]

    def gather(slot, base, stride, pace):
        small = piece // 2
        from_core = []

        def rows(zz, offset=0, count=piece):
            return pl.ds(pl.multiple_of(base + zz * stride + offset, 8), count)

        def send(target, zz, offset=0, count=piece):
            mine = full.at[slot, rows(zz, offset, count)]
            return copy(mine, mine, target)

        for step in range(reach):
            if step:
                going_up.wait_recv()
                going_down.wait_recv()
            if step == reach - 1:
                going_up = send(to_up, down(step), 0, small)
                going_down = send(to_down, up(step), small, small)
            else:
                going_up = send(to_up, down(step))
                going_down = send(to_down, up(step))
            from_core.append(send(to_core, down(step)))
            if step:
                from_core.append(send(to_core, up(step)))
            yield pace
        going_up.wait_recv()
        going_down.wait_recv()
        from_core.append(send(to_core, down(reach)))
        yield 1.2
        for crossing in from_core:
            crossing.wait_recv()

    def first_margin(chunk):
        slot = chunk
        partial_sum(0, 1, chunk, slot)
        mine = pl.ds(pl.multiple_of(core * half, half), half)
        theirs = pl.ds(pl.multiple_of((1 - core) * half, half), half)
        crossing = copy(part.at[slot, theirs], core_in.at[chunk], to_core)
        yield 2.5
        crossing.wait_recv()
        part[slot, mine] = part[slot, mine] + core_in[chunk]
        yield from scatter(slot, core * half, piece, 3.2)
        here = pl.ds(pl.multiple_of(core * half + z * piece, 8), piece)
        crossing = copy(part.at[slot, here], y_in.at[chunk], to_y)
        yield 4.0
        crossing.wait_recv()
        full[slot, here] = part[slot, here] + y_in[chunk]
        yield from gather(slot, core * half, piece, 3.6)
        finish_first(chunk, slot)

    conditional = []

    def second_margin(chunk):
        slot = chunks + chunk
        if chunk == 0:
            for arriving in halo:
                arriving.wait_recv()
        partial_sum(1 + core, 2 - 2 * core, chunk, slot)
        yield from scatter(slot, 0, 2 * piece, 5.0)

        def here(c):
            return pl.ds(pl.multiple_of(z * 2 * piece + c * piece, 8), piece)

        arriving = [
            copy(part.at[slot, here(1 - core)], mix_in.at[chunk, 0], to_mix[0]),
            copy(part.at[slot, here(core)], mix_in.at[chunk, 1], to_mix[1]),
            copy(part.at[slot, here(1 - core)], mix_in.at[chunk, 2], to_mix[2]),
        ]
        last = prepare(part.at[slot, here(core)], mix_in.at[chunk, 3], to_mix[3])
        conditional.append(last)

        @pl.when(core == 1)
        def _():
            last.start()

        @pl.when(core == 0)
        def _():
            mix_in[chunk, 3] = part[slot, here(core)]

        yield 4.5
        for crossing in arriving:
            crossing.wait_recv()

        @pl.when(core == 1)
        def _():
            last.wait_recv()

        full[slot, here(core)] = (mix_in[chunk, 0] + mix_in[chunk, 1]) + (mix_in[chunk, 2] + mix_in[chunk, 3])
        yield from gather(slot, core * piece, 2 * piece, 3.6)
        finish_second(chunk, slot)

    order = []
    for chunk in range(chunks):
        order.append((2.0 + 0.8 * chunk, len(order), first_margin(chunk)))
    for chunk in range(chunks):
        order.append((25.0 + 0.8 * chunk, len(order), second_margin(chunk)))
    heapq.heapify(order)
    while order:
        when, n, steps = heapq.heappop(order)
        wait = next(steps, None)
        if wait is not None:
            heapq.heappush(order, (when + wait, n, steps))

    def apply(high_ref, low_ref):
        left = stack[...]
        short = jnp.concatenate([left[:own], left[2 * own:3 * own]], 0)
        pieces_re, pieces_im = [], []
        for chunk in range(chunks):
            both = pl.ds(chunk * wide, wide)
            with_high = dot(left, high_ref[:, both])
            with_low = dot(short, low_ref[:, both])
            by_re = with_high[:own] + (with_high[own:2 * own] + with_low[:own])
            by_im = with_high[2 * own:3 * own] + (with_high[3 * own:] + with_low[own:])
            pieces_re.append(by_re[:, :WIDTH] - by_im[:, WIDTH:])
            pieces_im.append(by_re[:, WIDTH:] + by_im[:, :WIDTH])
        return jnp.concatenate(pieces_re, 1), jnp.concatenate(pieces_im, 1)

    handed = prepare(rows_out, rows_in, to_next)

    @pl.when(ka == 0)
    def _():
        row = lax.broadcasted_iota(jnp.int32, (own, 2 * bands), 0) + pw * own
        column = lax.broadcasted_iota(jnp.int32, (own, 2 * bands), 1)
        one = (row == column).astype(F32)
        high, low = high_low(one)
        stack[...] = jnp.concatenate([high[:, :bands], low[:, :bands], high[:, bands:], low[:, bands:]], 0)

    @pl.when(ka > 0)
    def _():
        handed.wait_recv()
        high, low = high_low(rows_in[...])
        stack[...] = jnp.concatenate([high[:, :bands], low[:, :bands], high[:, bands:], low[:, bands:]], 0)

    line_re, line_im = apply(p_high, p_low)
    rows_out[:, :bands] = line_re
    rows_out[:, bands:] = line_im

    @pl.when(ka < ka_size - 1)
    def _():
        handed.start()

    out_ref[1, 0] = line_re
    out_ref[1, 1] = line_im
    line_re, line_im = apply(m0_high, m0_low)
    out_ref[0, 0] = line_re
    out_ref[0, 1] = line_im

    for made in started:
        made.wait_send()

    @pl.when(core == 1)
    def _():
        for made in conditional:
            made.wait_send()

    @pl.when(ka < ka_size - 1)
    def _():
        handed.wait_send()


def shards(ka_size, pw_size, states_re, states_im):
    _, bands, waves = states_re.shape
    zsize = pw_size // 4
    own = bands // pw_size
    chunks = bands // WIDTH
    slots = 2 * chunks
    wide = 2 * WIDTH
    half = bands // 2
    piece = half // zsize
    reach = zsize // 2
    any_space = pl.BlockSpec(memory_space=pl.ANY)
    lines = pl.pallas_call(
        functools.partial(kernel, ka_size, zsize),
        out_shape=jax.ShapeDtypeStruct((2, 2, own, bands), F32),
        in_specs=[any_space, any_space],
        out_specs=pl.BlockSpec(memory_space=pltpu.VMEM),
        scratch_shapes=[
            pltpu.VMEM((3, bands, waves), BF16),
            pltpu.VMEM((3, bands, waves), BF16),
            pltpu.VMEM((slots, bands, wide), F32),
            pltpu.VMEM((chunks, half, wide), F32),
            pltpu.VMEM((slots, reach, 2 * piece, wide), F32),
            pltpu.VMEM((slots, reach, 2 * piece, wide), F32),
            pltpu.VMEM((chunks, piece, wide), F32),
            pltpu.VMEM((chunks, 4, piece, wide), F32),
            pltpu.VMEM((slots, bands, wide), F32),
            pltpu.VMEM((4, bands, bands), BF16),
            pltpu.VMEM((bands, 2 * bands), BF16),
            pltpu.VMEM((bands, 2 * bands), BF16),
            pltpu.VMEM((bands, 2 * bands), BF16),
            pltpu.VMEM((bands, 2 * bands), BF16),
            pltpu.VMEM((own, 2 * bands), F32),
            pltpu.VMEM((own, 2 * bands), F32),
            pltpu.VMEM((4 * own, bands), BF16),
            pltpu.SemaphoreType.DMA((2,)),
            pltpu.SemaphoreType.DMA((SEMS,)),
            pltpu.SemaphoreType.DMA((SEMS,)),
        ],
        compiler_params=pltpu.CompilerParams(
            collective_id=0, has_side_effects=True, vmem_limit_bytes=56 * 1024 * 1024
        ),
    )(states_re, states_im)
    return jnp.transpose(lines, (0, 2, 1, 3))


def solution(mesh):
    in_specs = (P("ka", None, "pw"), P("ka", None, "pw"))
    out_specs = P("ka", "pw", None, None)
    body = functools.partial(shards, mesh.shape["ka"], mesh.shape["pw"])
    return jax.shard_map(body, mesh=mesh, in_specs=in_specs, out_specs=out_specs, check_vma=False)
```

```python
import functools
import heapq

import jax
import jax.numpy as jnp
from jax import lax
from jax.experimental import pallas as pl
from jax.experimental.pallas import tpu as pltpu
from jax.sharding import PartitionSpec as P

F32 = jnp.float32
BF16 = jnp.bfloat16
WIDTH = 128
SEMS = 256
DEPTH = 2
FIRST_START = 2.0
FIRST_PACE = 1.5
GATHER_START = 32.0
SPREAD_PACE = 1.5
IN_TWO = (0, 1, 2, 3)
FINAL_PACE = 4.0
SUM_PACE = 4.2
HALO_START = 8.0
HALO_PACE = 5.8


def high_low(value):
    high = value.astype(BF16)
    return high, (value - high.astype(F32)).astype(BF16)


def dot(left, right):
    return jnp.dot(left, right, preferred_element_type=F32)


def dot_t(left, right):
    return lax.dot_general(left, right, (((1,), (1,)), ((), ())), preferred_element_type=F32)


def kernel(
    ka_size, zsize,
    re_hbm, im_hbm, out_ref,
    st, part0, part1, core_in, plus0, minus0, plus1, minus1, y_in, mix_columns, mix_rows, full0, full1,
    lhs0, m0_high, m0_low, p_high, p_low, rows_in, rows_out, stack,
    load_sem, send_sem, recv_sem,
):
    chunks, waves = st.shape[1], st.shape[4]
    bands = chunks * WIDTH
    wide = 2 * WIDTH
    half = bands // 2
    piece = half // zsize
    strip = WIDTH // zsize
    thin = strip // 2
    reach = zsize // 2
    own = rows_in.shape[0]

    ka = lax.axis_index("ka")
    pw = lax.axis_index("pw")
    core = lax.rem(pw, 2)
    z = lax.rem(pw // 2, zsize)
    yhi = pw // (2 * zsize)

    def device(k, y, zz, c):
        return {"ka": lax.rem(k + ka_size, ka_size), "pw": (y * zsize + zz) * 2 + c}

    def up(n):
        return lax.rem(z + n, zsize)

    def down(n):
        return lax.rem(z + zsize - n, zsize)

    to_core = device(ka, yhi, z, 1 - core)
    to_up = device(ka, yhi, up(1), core)
    to_down = device(ka, yhi, down(1), core)
    to_up2 = device(ka, yhi, up(2), core)
    to_down2 = device(ka, yhi, down(2), core)
    to_y = device(ka, 1 - yhi, z, core)
    to_next = device(ka + 1, yhi, z, core)
    to_prev = device(ka - 1, yhi, z, core)
    to_halo = device(ka - 1 + 2 * core, yhi, z, core)
    from_halo = device(ka + 1 - 2 * core, yhi, z, core)
    to_mix = (
        device(ka - core, yhi, z, 1 - core),
        device(ka - core, 1 - yhi, z, core),
        device(ka - core, 1 - yhi, z, 1 - core),
        to_prev,
    )
    from_mix = (
        device(ka + 1 - core, yhi, z, 1 - core),
        device(ka + core, 1 - yhi, z, core),
        device(ka + 1 - core, 1 - yhi, z, 1 - core),
        to_next,
    )

    loads = []
    for block in range(chunks):
        rows = pl.ds(block * WIDTH, WIDTH)
        for k in range(2):
            for n, hbm in enumerate((re_hbm, im_hbm)):
                loads.append(pltpu.make_async_copy(hbm.at[k, rows], st.at[k, block, n], load_sem.at[len(loads)]))
    for load in loads:
        load.start()

    barrier = pltpu.get_barrier_semaphore()
    senders = (to_core, to_up, to_down, to_y, to_prev, from_halo) + from_mix
    if reach == 4:
        senders += (to_up2, to_down2)
    for sender in senders:
        pl.semaphore_signal(barrier, inc=1, device_id=sender, device_id_type=pl.DeviceIdType.MESH)
    pl.semaphore_wait(barrier, len(senders))

    started = []
    numbered = [0]

    def prepare(src, dst, target, number=None):
        if number is None:
            number = numbered[0]
            numbered[0] += 1
        return pltpu.make_async_remote_copy(
            src_ref=src, dst_ref=dst, send_sem=send_sem.at[number], recv_sem=recv_sem.at[number],
            device_id=target, device_id_type=pl.DeviceIdType.MESH,
        )

    def copy(src, dst, target):
        made = prepare(src, dst, target)
        made.start()
        started.append(made)
        return made

    halo = []

    def states_across():
        for block in range(chunks):
            if block >= DEPTH:
                for made in halo[block - DEPTH]:
                    made.wait_send()
            rows = pl.ds(block * WIDTH, WIDTH)
            pair = [
                prepare(hbm.at[core, rows], st.at[2, block, n], to_halo) for n, hbm in enumerate((re_hbm, im_hbm))
            ]
            for made in pair:
                made.start()
            halo.append(pair)
            if block + 1 >= DEPTH:
                yield HALO_PACE
        for block in range(max(chunks - DEPTH, 0), chunks):
            for made in halo[block]:
                made.wait_send()

    def block_sum(left, right):
        both = dot_t(left.reshape(wide, waves), right.reshape(wide, waves))
        real = both[:WIDTH, :WIDTH] + both[WIDTH:, WIDTH:]
        imag = both[:WIDTH, WIDTH:] - both[WIDTH:, :WIDTH]
        return real, imag

    def finish_first(chunk):
        columns = pl.ds(chunk * WIDTH, WIDTH)
        both = pl.ds(chunk * wide, wide)
        high, low = high_low(full0[chunk])
        m0_high[:, both] = high
        m0_low[:, both] = low
        lhs0[0, :, columns] = high[:, :WIDTH]
        lhs0[1, :, columns] = low[:, :WIDTH]
        lhs0[2, :, columns] = high[:, WIDTH:]
        lhs0[3, :, columns] = low[:, WIDTH:]

    def finish_second(chunk):
        both = pl.ds(chunk * wide, wide)
        high, low = high_low(full1[chunk].reshape(bands, wide))

        @pl.loop(0, chunks)
        def _(step):
            rows = pl.ds(pl.multiple_of(step * WIDTH, WIDTH), WIDTH)
            re_high, re_low = lhs0[0, rows], lhs0[1, rows]
            im_high, im_low = lhs0[2, rows], lhs0[3, rows]
            by_re = dot(re_high, high) + (dot(re_low, high) + dot(re_high, low))
            by_im = dot(im_high, high) + (dot(im_low, high) + dot(im_high, low))
            new_re = by_re[:, :WIDTH] - by_im[:, WIDTH:]
            new_im = by_re[:, WIDTH:] + by_im[:, :WIDTH]
            span_high, span_low = high_low(jnp.concatenate([new_re, new_im], 1))
            p_high[rows, both] = span_high
            p_low[rows, both] = span_low

    def scatter(part, at, plus, minus, arrived, pace):
        def add(where, buffer, which):
            part[where] = part[where] + buffer[which]

        far = up(reach)
        going_up = copy(part.at[at(far, 0)], plus.at[arrived(0, 0)], to_up)
        going_down = copy(part.at[at(far, 1)], minus.at[arrived(0, 1)], to_down)
        yield pace
        for step in range(1, reach):
            going_up.wait_recv()
            going_down.wait_recv()
            there_up, there_down = up(reach - step), down(reach - step)
            if step == 1:
                add(at(there_up, 0), plus, arrived(0, 0))
                add(at(there_down, 1), minus, arrived(0, 1))
            else:
                add(at(there_up), plus, arrived(step - 1))
                add(at(there_down), minus, arrived(step - 1))
            going_up = copy(part.at[at(there_up)], plus.at[arrived(step)], to_up)
            going_down = copy(part.at[at(there_down)], minus.at[arrived(step)], to_down)
            yield pace
        going_up.wait_recv()
        going_down.wait_recv()
        if reach == 1:
            add(at(z, 0), plus, arrived(0, 0))
            add(at(z, 1), minus, arrived(0, 1))
        else:
            here = at(z)
            part[here] = part[here] + plus[arrived(reach - 1)] + minus[arrived(reach - 1)]

    def gather(full, at, pace):
        from_core = []

        def send(target, *which):
            mine = full.at[at(*which)]
            return copy(mine, mine, target)

        for step in range(reach):
            if step:
                going_up.wait_recv()
                going_down.wait_recv()
            if step == reach - 1:
                going_up = send(to_up, down(step), 0)
                going_down = send(to_down, up(step), 1)
            else:
                going_up = send(to_up, down(step))
                going_down = send(to_down, up(step))
            from_core.append(send(to_core, down(step)))
            if step:
                from_core.append(send(to_core, up(step)))
            yield pace
        going_up.wait_recv()
        going_down.wait_recv()
        from_core.append(send(to_core, down(reach)))
        yield 1.2
        for crossing in from_core:
            crossing.wait_recv()

    def gather_in_two(full, at, pace):
        def send(target, *which):
            mine = full.at[at(*which)]
            return copy(mine, mine, target)

        two_up, two_down = send(to_up2, z), send(to_down2, z)
        one_up, one_down = send(to_up, z), send(to_down, z)
        from_core = [send(to_core, z)]
        yield pace
        two_up.wait_recv()
        later = [send(to_up2, down(2), 0), send(to_up, down(2))]
        two_down.wait_recv()
        later += [send(to_down2, up(2), 1), send(to_down, up(2))]
        from_core += [send(to_core, down(2)), send(to_core, up(2))]
        one_up.wait_recv()
        one_down.wait_recv()
        from_core += [send(to_core, down(1)), send(to_core, up(1))]
        yield pace
        later[1].wait_recv()
        later[3].wait_recv()
        from_core += [send(to_core, down(3)), send(to_core, up(3))]
        later[0].wait_recv()
        later[2].wait_recv()
        from_core.append(send(to_core, up(4)))
        yield 2.0
        for crossing in from_core:
            crossing.wait_recv()

    def first_margin(chunk):
        if chunk == 0:
            for load in loads:
                load.wait()

        @pl.loop(0, chunks)
        def _(block):
            rows = pl.ds(pl.multiple_of(block * WIDTH, WIDTH), WIDTH)
            real, imag = block_sum(st[0, block], st[1, chunk])
            part0[chunk, rows, :WIDTH] = real
            part0[chunk, rows, WIDTH:] = imag

        mine = pl.ds(pl.multiple_of(core * half, half), half)
        theirs = pl.ds(pl.multiple_of((1 - core) * half, half), half)
        crossing = copy(part0.at[chunk, theirs], core_in.at[chunk], to_core)
        yield 2.5
        crossing.wait_recv()
        part0[chunk, mine] = part0[chunk, mine] + core_in[chunk]

        def at(zz, h=None):
            count = piece if h is None else piece // 2
            start = core * half + zz * piece + (h or 0) * count
            return chunk, pl.ds(pl.multiple_of(start, 8), count)

        def arrived(step, h=None):
            count = piece if h is None else piece // 2
            return chunk, step, pl.ds((h or 0) * count, count)

        yield from scatter(part0, at, plus0, minus0, arrived, 3.2)
        crossing = copy(part0.at[at(z)], y_in.at[chunk], to_y)
        yield GATHER_START - (FIRST_START + 15.3)
        crossing.wait_recv()
        full0[at(z)] = part0[at(z)] + y_in[chunk]
        yield from gather(full0, at, 3.6)
        finish_first(chunk)

    def blocks_of(h):
        return pl.ds(0, chunks) if h is None else pl.ds(h * (chunks // 2), chunks // 2)

    def second_margin(chunk):
        for arriving in halo[chunk]:
            arriving.wait_recv()

        @pl.loop(0, chunks)
        def _(block):
            left_block = block * (1 - core) + chunk * core
            right_block = block * core + chunk * (1 - core)
            real, imag = block_sum(st[1 + core, left_block], st[2 - 2 * core, right_block])
            part1[chunk, block, :, :WIDTH] = real
            part1[chunk, block, :, WIDTH:] = imag

        def at(zz, h=None):
            return chunk, blocks_of(h), pl.ds(pl.multiple_of(zz * strip, 8), strip)

        def arrived(step, h=None):
            return chunk, step, blocks_of(h)

        yield from scatter(part1, at, plus1, minus1, arrived, SUM_PACE)

        def rows(c):
            return chunk, slice(None), pl.ds(pl.multiple_of(z * strip + c * thin, 8), thin)

        number = numbered[0]
        numbered[0] += 4
        ways = ((1 - core, 0), (core, 1), (1 - core, 1), (core, 0))
        from_zero = [
            prepare(part1.at[rows(c)], mix_columns.at[chunk, far], to_mix[n], number + n)
            for n, (c, far) in enumerate(ways[:3])
        ]
        from_one = [
            prepare(part1.at[rows(c)], mix_rows.at[chunk, far], to_mix[n], number + n)
            for n, (c, far) in enumerate(ways)
        ]
        joined.extend(from_zero)
        conditional.append(from_one[3])

        @pl.when(core == 0)
        def _():
            for made in from_zero:
                made.start()
            mix_columns[chunk, 0] = part1[rows(core)]

        @pl.when(core == 1)
        def _():
            for made in from_one:
                made.start()

        yield 4.5
        for made in from_zero:
            made.wait_recv()

        @pl.when(core == 1)
        def _():
            from_one[3].wait_recv()

    conditional = []
    joined = []

    def spread(chunk):
        def at(zz, h=None):
            return chunk, blocks_of(h), pl.ds(pl.multiple_of(zz * strip + core * thin, 8), thin)

        full1[at(z)] = (mix_columns[chunk, 0] + mix_columns[chunk, 1]) + (mix_rows[:, 0, chunk] + mix_rows[:, 1, chunk])
        if reach == 4 and chunk in IN_TWO:
            yield from gather_in_two(full1, at, FINAL_PACE)
        else:
            yield from gather(full1, at, 3.6)
        assert firsts == chunks
        finish_second(chunk)

    order = [(0.0, 0, "halo", states_across())]
    for chunk in range(chunks):
        order.append((FIRST_START + FIRST_PACE * chunk, len(order), "first", first_margin(chunk)))
    for chunk in range(chunks):
        order.append((HALO_START + HALO_PACE * chunk, len(order), "second", second_margin(chunk)))
    heapq.heapify(order)
    firsts = seconds = 0
    while order:
        when, n, kind, steps = heapq.heappop(order)
        wait = next(steps, None)
        if wait is not None:
            heapq.heappush(order, (when + wait, n, kind, steps))
        firsts += wait is None and kind == "first"
        seconds += wait is None and kind == "second"
        if wait is None and kind == "second" and seconds == chunks:
            for chunk in range(chunks):
                heapq.heappush(order, (when + SPREAD_PACE * chunk, 100 + chunk, "spread", spread(chunk)))

    def apply(high_ref, low_ref):
        left = stack[...]
        short = jnp.concatenate([left[:own], left[2 * own:3 * own]], 0)
        pieces_re, pieces_im = [], []
        for chunk in range(chunks):
            both = pl.ds(chunk * wide, wide)
            with_high = dot(left, high_ref[:, both])
            with_low = dot(short, low_ref[:, both])
            by_re = with_high[:own] + (with_high[own:2 * own] + with_low[:own])
            by_im = with_high[2 * own:3 * own] + (with_high[3 * own:] + with_low[own:])
            pieces_re.append(by_re[:, :WIDTH] - by_im[:, WIDTH:])
            pieces_im.append(by_re[:, WIDTH:] + by_im[:, :WIDTH])
        return jnp.concatenate(pieces_re, 1), jnp.concatenate(pieces_im, 1)

    handed = prepare(rows_out, rows_in, to_next)

    @pl.when(ka == 0)
    def _():
        row = lax.broadcasted_iota(jnp.int32, (own, 2 * bands), 0) + pw * own
        column = lax.broadcasted_iota(jnp.int32, (own, 2 * bands), 1)
        one = (row == column).astype(F32)
        high, low = high_low(one)
        stack[...] = jnp.concatenate([high[:, :bands], low[:, :bands], high[:, bands:], low[:, bands:]], 0)

    @pl.when(ka > 0)
    def _():
        handed.wait_recv()
        high, low = high_low(rows_in[...])
        stack[...] = jnp.concatenate([high[:, :bands], low[:, :bands], high[:, bands:], low[:, bands:]], 0)

    line_re, line_im = apply(p_high, p_low)
    rows_out[:, :bands] = line_re
    rows_out[:, bands:] = line_im

    @pl.when(ka < ka_size - 1)
    def _():
        handed.start()

    out_ref[1, 0] = line_re
    out_ref[1, 1] = line_im
    line_re, line_im = apply(m0_high, m0_low)
    out_ref[0, 0] = line_re
    out_ref[0, 1] = line_im

    for made in started + joined:
        made.wait_send()

    @pl.when(core == 1)
    def _():
        for made in conditional:
            made.wait_send()

    @pl.when(ka < ka_size - 1)
    def _():
        handed.wait_send()


def shards(ka_size, pw_size, states_re, states_im):
    _, bands, waves = states_re.shape
    zsize = pw_size // 4
    own = bands // pw_size
    chunks = bands // WIDTH
    strip = WIDTH // zsize
    wide = 2 * WIDTH
    half = bands // 2
    piece = half // zsize
    reach = zsize // 2
    any_space = pl.BlockSpec(memory_space=pl.ANY)
    lines = pl.pallas_call(
        functools.partial(kernel, ka_size, zsize),
        out_shape=jax.ShapeDtypeStruct((2, 2, own, bands), F32),
        in_specs=[any_space, any_space],
        out_specs=pl.BlockSpec(memory_space=pltpu.VMEM),
        scratch_shapes=[
            pltpu.VMEM((3, chunks, 2, WIDTH, waves), BF16),
            pltpu.VMEM((chunks, bands, wide), F32),
            pltpu.VMEM((chunks, chunks, WIDTH, wide), F32),
            pltpu.VMEM((chunks, half, wide), F32),
            pltpu.VMEM((chunks, reach, piece, wide), F32),
            pltpu.VMEM((chunks, reach, piece, wide), F32),
            pltpu.VMEM((chunks, reach, chunks, strip, wide), F32),
            pltpu.VMEM((chunks, reach, chunks, strip, wide), F32),
            pltpu.VMEM((chunks, piece, wide), F32),
            pltpu.VMEM((chunks, 2, chunks, strip // 2, wide), F32),
            pltpu.VMEM((chunks, 2, chunks, strip // 2, wide), F32),
            pltpu.VMEM((chunks, bands, wide), F32),
            pltpu.VMEM((chunks, chunks, WIDTH, wide), F32),
            pltpu.VMEM((4, bands, bands), BF16),
            pltpu.VMEM((bands, 2 * bands), BF16),
            pltpu.VMEM((bands, 2 * bands), BF16),
            pltpu.VMEM((bands, 2 * bands), BF16),
            pltpu.VMEM((bands, 2 * bands), BF16),
            pltpu.VMEM((own, 2 * bands), F32),
            pltpu.VMEM((own, 2 * bands), F32),
            pltpu.VMEM((4 * own, bands), BF16),
            pltpu.SemaphoreType.DMA((4 * chunks,)),
            pltpu.SemaphoreType.DMA((SEMS,)),
            pltpu.SemaphoreType.DMA((SEMS,)),
        ],
        compiler_params=pltpu.CompilerParams(
            collective_id=0, has_side_effects=True, vmem_limit_bytes=56 * 1024 * 1024
        ),
    )(states_re, states_im)
    return jnp.transpose(lines, (0, 2, 1, 3))


def solution(mesh):
    in_specs = (P("ka", None, "pw"), P("ka", None, "pw"))
    out_specs = P("ka", "pw", None, None)
    body = functools.partial(shards, mesh.shape["ka"], mesh.shape["pw"])
    return jax.shard_map(body, mesh=mesh, in_specs=in_specs, out_specs=out_specs, check_vma=False)
```

```python
import functools
import heapq

import jax
import jax.numpy as jnp
from jax import lax
from jax.experimental import pallas as pl
from jax.experimental.pallas import tpu as pltpu
from jax.sharding import PartitionSpec as P

F32 = jnp.float32
BF16 = jnp.bfloat16
WIDTH = 128
SEMS = 256
DEPTH = 2
FIRST_START = 2.0
FIRST_PACE = 1.5
GATHER_START = 32.0
SPREAD_PACE = 1.5
IN_TWO = (0, 1, 2, 3)
FINAL_PACE = 4.0
SUM_PACE = 4.2
HALO_START = 8.0
HALO_PACE = 5.8


def high_low(value):
    high = value.astype(BF16)
    return high, (value - high.astype(F32)).astype(BF16)


def dot(left, right):
    return jnp.dot(left, right, preferred_element_type=F32)


def dot_t(left, right):
    return lax.dot_general(left, right, (((1,), (1,)), ((), ())), preferred_element_type=F32)


def kernel(
    ka_size, zsize,
    re_hbm, im_hbm, out_ref,
    st, part0, part1, core_in, plus0, minus0, plus1, minus1, y_in, mix_columns, mix_rows, full0, full1,
    lhs0, m0_high, m0_low, p_high, p_low, rows_in, rows_out, stack,
    load_sem, send_sem, recv_sem,
):
    chunks, waves = st.shape[1], st.shape[4]
    bands = chunks * WIDTH
    wide = 2 * WIDTH
    half = bands // 2
    piece = half // zsize
    strip = WIDTH // zsize
    thin = strip // 2
    reach = zsize // 2
    own = rows_in.shape[1]

    ka = lax.axis_index("ka")
    pw = lax.axis_index("pw")
    core = lax.rem(pw, 2)
    z = lax.rem(pw // 2, zsize)
    yhi = pw // (2 * zsize)

    def device(k, y, zz, c):
        return {"ka": lax.rem(k + ka_size, ka_size), "pw": (y * zsize + zz) * 2 + c}

    def up(n):
        return lax.rem(z + n, zsize)

    def down(n):
        return lax.rem(z + zsize - n, zsize)

    to_core = device(ka, yhi, z, 1 - core)
    to_up = device(ka, yhi, up(1), core)
    to_down = device(ka, yhi, down(1), core)
    to_up2 = device(ka, yhi, up(2), core)
    to_down2 = device(ka, yhi, down(2), core)
    to_y = device(ka, 1 - yhi, z, core)
    to_next = device(ka + 1, yhi, z, core)
    to_prev = device(ka - 1, yhi, z, core)
    to_halo = device(ka - 1 + 2 * core, yhi, z, core)
    from_halo = device(ka + 1 - 2 * core, yhi, z, core)
    to_mix = (
        device(ka - core, yhi, z, 1 - core),
        device(ka - core, 1 - yhi, z, core),
        device(ka - core, 1 - yhi, z, 1 - core),
        to_prev,
    )
    from_mix = (
        device(ka + 1 - core, yhi, z, 1 - core),
        device(ka + core, 1 - yhi, z, core),
        device(ka + 1 - core, 1 - yhi, z, 1 - core),
        to_next,
    )

    loads = []
    for block in range(chunks):
        rows = pl.ds(block * WIDTH, WIDTH)
        for k in range(2):
            for n, hbm in enumerate((re_hbm, im_hbm)):
                loads.append(pltpu.make_async_copy(hbm.at[k, rows], st.at[k, block, n], load_sem.at[len(loads)]))
    for load in loads:
        load.start()

    barrier = pltpu.get_barrier_semaphore()
    senders = (to_core, to_up, to_down, to_y, to_prev, from_halo) + from_mix
    if reach == 4:
        senders += (to_up2, to_down2)
    for sender in senders:
        pl.semaphore_signal(barrier, inc=1, device_id=sender, device_id_type=pl.DeviceIdType.MESH)
    pl.semaphore_wait(barrier, len(senders))

    started = []
    numbered = [0]

    def prepare(src, dst, target, number=None):
        if number is None:
            number = numbered[0]
            numbered[0] += 1
        return pltpu.make_async_remote_copy(
            src_ref=src, dst_ref=dst, send_sem=send_sem.at[number], recv_sem=recv_sem.at[number],
            device_id=target, device_id_type=pl.DeviceIdType.MESH,
        )

    def copy(src, dst, target):
        made = prepare(src, dst, target)
        made.start()
        started.append(made)
        return made

    halo = []

    def states_across():
        for block in range(chunks):
            if block >= DEPTH:
                for made in halo[block - DEPTH]:
                    made.wait_send()
            rows = pl.ds(block * WIDTH, WIDTH)
            pair = [
                prepare(hbm.at[core, rows], st.at[2, block, n], to_halo) for n, hbm in enumerate((re_hbm, im_hbm))
            ]
            for made in pair:
                made.start()
            halo.append(pair)
            if block + 1 >= DEPTH:
                yield HALO_PACE
        for block in range(max(chunks - DEPTH, 0), chunks):
            for made in halo[block]:
                made.wait_send()

    def block_sum(left, right):
        both = dot_t(left.reshape(wide, waves), right.reshape(wide, waves))
        real = both[:WIDTH, :WIDTH] + both[WIDTH:, WIDTH:]
        imag = both[:WIDTH, WIDTH:] - both[WIDTH:, :WIDTH]
        return real, imag

    def finish_first(chunk):
        columns = pl.ds(chunk * WIDTH, WIDTH)
        both = pl.ds(chunk * wide, wide)
        high, low = high_low(full0[chunk])
        m0_high[:, both] = high
        m0_low[:, both] = low
        lhs0[0, :, columns] = high[:, :WIDTH]
        lhs0[1, :, columns] = low[:, :WIDTH]
        lhs0[2, :, columns] = high[:, WIDTH:]
        lhs0[3, :, columns] = low[:, WIDTH:]

    def finish_second(chunk):
        both = pl.ds(chunk * wide, wide)
        high, low = high_low(full1[chunk].reshape(bands, wide))

        @pl.loop(0, chunks)
        def _(step):
            rows = pl.ds(pl.multiple_of(step * WIDTH, WIDTH), WIDTH)
            re_high, re_low = lhs0[0, rows], lhs0[1, rows]
            im_high, im_low = lhs0[2, rows], lhs0[3, rows]
            by_re = dot(re_high, high) + (dot(re_low, high) + dot(re_high, low))
            by_im = dot(im_high, high) + (dot(im_low, high) + dot(im_high, low))
            new_re = by_re[:, :WIDTH] - by_im[:, WIDTH:]
            new_im = by_re[:, WIDTH:] + by_im[:, :WIDTH]
            span_high, span_low = high_low(jnp.concatenate([new_re, new_im], 1))
            p_high[rows, both] = span_high
            p_low[rows, both] = span_low

    def scatter(part, at, plus, minus, arrived, pace):
        def add(where, buffer, which):
            part[where] = part[where] + buffer[which]

        far = up(reach)
        going_up = copy(part.at[at(far, 0)], plus.at[arrived(0, 0)], to_up)
        going_down = copy(part.at[at(far, 1)], minus.at[arrived(0, 1)], to_down)
        yield pace
        for step in range(1, reach):
            going_up.wait_recv()
            going_down.wait_recv()
            there_up, there_down = up(reach - step), down(reach - step)
            if step == 1:
                add(at(there_up, 0), plus, arrived(0, 0))
                add(at(there_down, 1), minus, arrived(0, 1))
            else:
                add(at(there_up), plus, arrived(step - 1))
                add(at(there_down), minus, arrived(step - 1))
            going_up = copy(part.at[at(there_up)], plus.at[arrived(step)], to_up)
            going_down = copy(part.at[at(there_down)], minus.at[arrived(step)], to_down)
            yield pace
        going_up.wait_recv()
        going_down.wait_recv()
        if reach == 1:
            add(at(z, 0), plus, arrived(0, 0))
            add(at(z, 1), minus, arrived(0, 1))
        else:
            here = at(z)
            part[here] = part[here] + plus[arrived(reach - 1)] + minus[arrived(reach - 1)]

    def gather(full, at, pace):
        from_core = []

        def send(target, *which):
            mine = full.at[at(*which)]
            return copy(mine, mine, target)

        for step in range(reach):
            if step:
                going_up.wait_recv()
                going_down.wait_recv()
            if step == reach - 1:
                going_up = send(to_up, down(step), 0)
                going_down = send(to_down, up(step), 1)
            else:
                going_up = send(to_up, down(step))
                going_down = send(to_down, up(step))
            from_core.append(send(to_core, down(step)))
            if step:
                from_core.append(send(to_core, up(step)))
            yield pace
        going_up.wait_recv()
        going_down.wait_recv()
        from_core.append(send(to_core, down(reach)))
        yield 1.2
        for crossing in from_core:
            crossing.wait_recv()

    def gather_in_two(full, at, pace):
        def send(target, *which):
            mine = full.at[at(*which)]
            return copy(mine, mine, target)

        two_up, two_down = send(to_up2, z), send(to_down2, z)
        one_up, one_down = send(to_up, z), send(to_down, z)
        from_core = [send(to_core, z)]
        yield pace
        two_up.wait_recv()
        later = [send(to_up2, down(2), 0), send(to_up, down(2))]
        two_down.wait_recv()
        later += [send(to_down2, up(2), 1), send(to_down, up(2))]
        from_core += [send(to_core, down(2)), send(to_core, up(2))]
        one_up.wait_recv()
        one_down.wait_recv()
        from_core += [send(to_core, down(1)), send(to_core, up(1))]
        yield pace
        later[1].wait_recv()
        later[3].wait_recv()
        from_core += [send(to_core, down(3)), send(to_core, up(3))]
        later[0].wait_recv()
        later[2].wait_recv()
        from_core.append(send(to_core, up(4)))
        yield 2.0
        for crossing in from_core:
            crossing.wait_recv()

    def first_margin(chunk):
        if chunk == 0:
            for load in loads:
                load.wait()

        @pl.loop(0, chunks)
        def _(block):
            rows = pl.ds(pl.multiple_of(block * WIDTH, WIDTH), WIDTH)
            real, imag = block_sum(st[0, block], st[1, chunk])
            part0[chunk, rows, :WIDTH] = real
            part0[chunk, rows, WIDTH:] = imag

        mine = pl.ds(pl.multiple_of(core * half, half), half)
        theirs = pl.ds(pl.multiple_of((1 - core) * half, half), half)
        crossing = copy(part0.at[chunk, theirs], core_in.at[chunk], to_core)
        yield 2.5
        crossing.wait_recv()
        part0[chunk, mine] = part0[chunk, mine] + core_in[chunk]

        def at(zz, h=None):
            count = piece if h is None else piece // 2
            start = core * half + zz * piece + (h or 0) * count
            return chunk, pl.ds(pl.multiple_of(start, 8), count)

        def arrived(step, h=None):
            count = piece if h is None else piece // 2
            return chunk, step, pl.ds((h or 0) * count, count)

        yield from scatter(part0, at, plus0, minus0, arrived, 3.2)
        crossing = copy(part0.at[at(z)], y_in.at[chunk], to_y)
        yield GATHER_START - (FIRST_START + 15.3)
        crossing.wait_recv()
        full0[at(z)] = part0[at(z)] + y_in[chunk]
        yield from gather(full0, at, 3.6)
        finish_first(chunk)

    def blocks_of(h):
        return pl.ds(0, chunks) if h is None else pl.ds(h * (chunks // 2), chunks // 2)

    def second_margin(chunk):
        for arriving in halo[chunk]:
            arriving.wait_recv()

        @pl.loop(0, chunks)
        def _(block):
            left_block = block * (1 - core) + chunk * core
            right_block = block * core + chunk * (1 - core)
            real, imag = block_sum(st[1 + core, left_block], st[2 - 2 * core, right_block])
            part1[chunk, block, :, :WIDTH] = real
            part1[chunk, block, :, WIDTH:] = imag

        def at(zz, h=None):
            return chunk, blocks_of(h), pl.ds(pl.multiple_of(zz * strip, 8), strip)

        def arrived(step, h=None):
            return chunk, step, blocks_of(h)

        yield from scatter(part1, at, plus1, minus1, arrived, SUM_PACE)

        def rows(c):
            return chunk, slice(None), pl.ds(pl.multiple_of(z * strip + c * thin, 8), thin)

        number = numbered[0]
        numbered[0] += 4
        ways = ((1 - core, 0), (core, 1), (1 - core, 1), (core, 0))
        from_zero = [
            prepare(part1.at[rows(c)], mix_columns.at[chunk, far], to_mix[n], number + n)
            for n, (c, far) in enumerate(ways[:3])
        ]
        from_one = [
            prepare(part1.at[rows(c)], mix_rows.at[chunk, far], to_mix[n], number + n)
            for n, (c, far) in enumerate(ways)
        ]
        joined.extend(from_zero)
        conditional.append(from_one[3])

        @pl.when(core == 0)
        def _():
            for made in from_zero:
                made.start()
            mix_columns[chunk, 0] = part1[rows(core)]

        @pl.when(core == 1)
        def _():
            for made in from_one:
                made.start()

        yield 4.5
        for made in from_zero:
            made.wait_recv()

        @pl.when(core == 1)
        def _():
            from_one[3].wait_recv()

    conditional = []
    joined = []

    def spread(chunk):
        def at(zz, h=None):
            return chunk, blocks_of(h), pl.ds(pl.multiple_of(zz * strip + core * thin, 8), thin)

        full1[at(z)] = (mix_columns[chunk, 0] + mix_columns[chunk, 1]) + (mix_rows[:, 0, chunk] + mix_rows[:, 1, chunk])
        if reach == 4 and chunk in IN_TWO:
            yield from gather_in_two(full1, at, FINAL_PACE)
        else:
            yield from gather(full1, at, 3.6)
        assert firsts == chunks
        finish_second(chunk)

    order = [(0.0, 0, "halo", states_across())]
    for chunk in range(chunks):
        order.append((FIRST_START + FIRST_PACE * chunk, len(order), "first", first_margin(chunk)))
    for chunk in range(chunks):
        order.append((HALO_START + HALO_PACE * chunk, len(order), "second", second_margin(chunk)))
    heapq.heapify(order)
    firsts = seconds = 0
    while order:
        when, n, kind, steps = heapq.heappop(order)
        wait = next(steps, None)
        if wait is not None:
            heapq.heappush(order, (when + wait, n, kind, steps))
        firsts += wait is None and kind == "first"
        seconds += wait is None and kind == "second"
        if wait is None and kind == "second" and seconds == chunks:
            for chunk in range(chunks):
                heapq.heappush(order, (when + SPREAD_PACE * chunk, 100 + chunk, "spread", spread(chunk)))

    def keep(h, value):
        high, low = high_low(value)
        stack[h] = jnp.concatenate([high[:, :half], low[:, :half], high[:, half:], low[:, half:]], 0)

    def product(high_ref, low_ref, h, chunk):
        deep, both = pl.ds(h * half, half), pl.ds(chunk * wide, wide)
        left = stack[h]
        short = jnp.concatenate([left[:own], left[2 * own:3 * own]], 0)
        with_high = dot(left, high_ref[deep, both])
        with_low = dot(short, low_ref[deep, both])
        by_re = with_high[:own] + (with_high[own:2 * own] + with_low[:own])
        by_im = with_high[2 * own:3 * own] + (with_high[3 * own:] + with_low[own:])
        return by_re[:, :WIDTH] - by_im[:, WIDTH:], by_re[:, WIDTH:] + by_im[:, :WIDTH]

    handed = [prepare(rows_out.at[h], rows_in.at[h], to_next) for h in range(2)]

    @pl.when(ka == 0)
    def _():
        for h in range(2):
            row = lax.broadcasted_iota(jnp.int32, (own, bands), 0) + pw * own
            column = lax.broadcasted_iota(jnp.int32, (own, bands), 1)
            keep(h, ((row == column + h * half) & (column < half)).astype(F32))

    @pl.when(ka > 0)
    def _():
        handed[0].wait_recv()
        keep(0, rows_in[0])

    begun = [product(p_high, p_low, 0, chunk) for chunk in range(chunks)]

    @pl.when(ka > 0)
    def _():
        handed[1].wait_recv()
        keep(1, rows_in[1])

    each = chunks // 2
    for h in range(2):
        for n in range(each):
            chunk = h * each + n
            more_re, more_im = product(p_high, p_low, 1, chunk)
            rows_out[h, :, pl.ds(n * WIDTH, WIDTH)] = begun[chunk][0] + more_re
            rows_out[h, :, pl.ds(half + n * WIDTH, WIDTH)] = begun[chunk][1] + more_im

        @pl.when(ka < ka_size - 1)
        def _():
            handed[h].start()

    for h in range(2):
        columns = pl.ds(h * half, half)
        out_ref[1, 0, :, columns] = rows_out[h, :, :half]
        out_ref[1, 1, :, columns] = rows_out[h, :, half:]
    for chunk in range(chunks):
        columns = pl.ds(chunk * WIDTH, WIDTH)
        first_re, first_im = product(m0_high, m0_low, 0, chunk)
        more_re, more_im = product(m0_high, m0_low, 1, chunk)
        out_ref[0, 0, :, columns] = first_re + more_re
        out_ref[0, 1, :, columns] = first_im + more_im

    for made in started + joined:
        made.wait_send()

    @pl.when(core == 1)
    def _():
        for made in conditional:
            made.wait_send()

    @pl.when(ka < ka_size - 1)
    def _():
        for made in handed:
            made.wait_send()


def shards(ka_size, pw_size, states_re, states_im):
    _, bands, waves = states_re.shape
    zsize = pw_size // 4
    own = bands // pw_size
    chunks = bands // WIDTH
    strip = WIDTH // zsize
    wide = 2 * WIDTH
    half = bands // 2
    piece = half // zsize
    reach = zsize // 2
    any_space = pl.BlockSpec(memory_space=pl.ANY)
    lines = pl.pallas_call(
        functools.partial(kernel, ka_size, zsize),
        out_shape=jax.ShapeDtypeStruct((2, 2, own, bands), F32),
        in_specs=[any_space, any_space],
        out_specs=pl.BlockSpec(memory_space=pltpu.VMEM),
        scratch_shapes=[
            pltpu.VMEM((3, chunks, 2, WIDTH, waves), BF16),
            pltpu.VMEM((chunks, bands, wide), F32),
            pltpu.VMEM((chunks, chunks, WIDTH, wide), F32),
            pltpu.VMEM((chunks, half, wide), F32),
            pltpu.VMEM((chunks, reach, piece, wide), F32),
            pltpu.VMEM((chunks, reach, piece, wide), F32),
            pltpu.VMEM((chunks, reach, chunks, strip, wide), F32),
            pltpu.VMEM((chunks, reach, chunks, strip, wide), F32),
            pltpu.VMEM((chunks, piece, wide), F32),
            pltpu.VMEM((chunks, 2, chunks, strip // 2, wide), F32),
            pltpu.VMEM((chunks, 2, chunks, strip // 2, wide), F32),
            pltpu.VMEM((chunks, bands, wide), F32),
            pltpu.VMEM((chunks, chunks, WIDTH, wide), F32),
            pltpu.VMEM((4, bands, bands), BF16),
            pltpu.VMEM((bands, 2 * bands), BF16),
            pltpu.VMEM((bands, 2 * bands), BF16),
            pltpu.VMEM((bands, 2 * bands), BF16),
            pltpu.VMEM((bands, 2 * bands), BF16),
            pltpu.VMEM((2, own, bands), F32),
            pltpu.VMEM((2, own, bands), F32),
            pltpu.VMEM((2, 4 * own, half), BF16),
            pltpu.SemaphoreType.DMA((4 * chunks,)),
            pltpu.SemaphoreType.DMA((SEMS,)),
            pltpu.SemaphoreType.DMA((SEMS,)),
        ],
        compiler_params=pltpu.CompilerParams(
            collective_id=0, has_side_effects=True, vmem_limit_bytes=56 * 1024 * 1024
        ),
    )(states_re, states_im)
    return jnp.transpose(lines, (0, 2, 1, 3))


def solution(mesh):
    in_specs = (P("ka", None, "pw"), P("ka", None, "pw"))
    out_specs = P("ka", "pw", None, None)
    body = functools.partial(shards, mesh.shape["ka"], mesh.shape["pw"])
    return jax.shard_map(body, mesh=mesh, in_specs=in_specs, out_specs=out_specs, check_vma=False)
```

```python
import functools
import heapq

import jax
import jax.numpy as jnp
from jax import lax
from jax.experimental import pallas as pl
from jax.experimental.pallas import tpu as pltpu
from jax.sharding import PartitionSpec as P

F32 = jnp.float32
BF16 = jnp.bfloat16
WIDTH = 128
SEMS = 256
DEPTH = 2
FIRST_START = 2.0
FIRST_PACE = 0.8
GATHER_START = 32.0
SPREAD_PACE = 1.5
IN_TWO = (0, 1, 2, 3)
FINAL_PACE = 4.0
SUM_PACE = 4.2
HALO_START = 8.0
HALO_PACE = 5.8


def high_low(value):
    high = value.astype(BF16)
    return high, (value - high.astype(F32)).astype(BF16)


def dot(left, right):
    return jnp.dot(left, right, preferred_element_type=F32)


def dot_t(left, right):
    return lax.dot_general(left, right, (((1,), (1,)), ((), ())), preferred_element_type=F32)


def kernel(
    ka_size, zsize,
    re_hbm, im_hbm, out_ref,
    st, part0, part1, core_in, plus0, minus0, plus1, minus1, y_in, mix_columns, mix_rows, full0, full1,
    lhs0, m0_high, m0_low, p_high, p_low, rows_in, rows_out, stack,
    load_sem, send_sem, recv_sem,
):
    chunks, waves = st.shape[1], st.shape[4]
    bands = chunks * WIDTH
    wide = 2 * WIDTH
    half = bands // 2
    piece = half // zsize
    strip = WIDTH // zsize
    thin = strip // 2
    reach = zsize // 2
    own = rows_in.shape[1]

    ka = lax.axis_index("ka")
    pw = lax.axis_index("pw")
    core = lax.rem(pw, 2)
    z = lax.rem(pw // 2, zsize)
    yhi = pw // (2 * zsize)

    def device(k, y, zz, c):
        return {"ka": lax.rem(k + ka_size, ka_size), "pw": (y * zsize + zz) * 2 + c}

    def up(n):
        return lax.rem(z + n, zsize)

    def down(n):
        return lax.rem(z + zsize - n, zsize)

    to_core = device(ka, yhi, z, 1 - core)
    to_up = device(ka, yhi, up(1), core)
    to_down = device(ka, yhi, down(1), core)
    to_up2 = device(ka, yhi, up(2), core)
    to_down2 = device(ka, yhi, down(2), core)
    to_y = device(ka, 1 - yhi, z, core)
    to_next = device(ka + 1, yhi, z, core)
    to_prev = device(ka - 1, yhi, z, core)
    to_halo = device(ka - 1 + 2 * core, yhi, z, core)
    from_halo = device(ka + 1 - 2 * core, yhi, z, core)
    to_mix = (
        device(ka - core, yhi, z, 1 - core),
        device(ka - core, 1 - yhi, z, core),
        device(ka - core, 1 - yhi, z, 1 - core),
        to_prev,
    )
    from_mix = (
        device(ka + 1 - core, yhi, z, 1 - core),
        device(ka + core, 1 - yhi, z, core),
        device(ka + 1 - core, 1 - yhi, z, 1 - core),
        to_next,
    )

    loads = []
    for block in range(chunks):
        rows = pl.ds(block * WIDTH, WIDTH)
        for k in range(2):
            for n, hbm in enumerate((re_hbm, im_hbm)):
                loads.append(pltpu.make_async_copy(hbm.at[k, rows], st.at[k, block, n], load_sem.at[len(loads)]))
    for load in loads:
        load.start()

    barrier = pltpu.get_barrier_semaphore()
    senders = (to_core, to_up, to_down, to_y, to_prev, from_halo) + from_mix
    if reach == 4:
        senders += (to_up2, to_down2)
    for sender in senders:
        pl.semaphore_signal(barrier, inc=1, device_id=sender, device_id_type=pl.DeviceIdType.MESH)
    pl.semaphore_wait(barrier, len(senders))

    started = []
    numbered = [0]

    def prepare(src, dst, target, number=None):
        if number is None:
            number = numbered[0]
            numbered[0] += 1
        return pltpu.make_async_remote_copy(
            src_ref=src, dst_ref=dst, send_sem=send_sem.at[number], recv_sem=recv_sem.at[number],
            device_id=target, device_id_type=pl.DeviceIdType.MESH,
        )

    def copy(src, dst, target):
        made = prepare(src, dst, target)
        made.start()
        started.append(made)
        return made

    halo = []

    def states_across():
        for block in range(chunks):
            if block >= DEPTH:
                for made in halo[block - DEPTH]:
                    made.wait_send()
            rows = pl.ds(block * WIDTH, WIDTH)
            pair = [
                prepare(hbm.at[core, rows], st.at[2, block, n], to_halo) for n, hbm in enumerate((re_hbm, im_hbm))
            ]
            for made in pair:
                made.start()
            halo.append(pair)
            if block + 1 >= DEPTH:
                yield HALO_PACE
        for block in range(max(chunks - DEPTH, 0), chunks):
            for made in halo[block]:
                made.wait_send()

    def block_sum(left, right):
        both = dot_t(left.reshape(wide, waves), right.reshape(wide, waves))
        real = both[:WIDTH, :WIDTH] + both[WIDTH:, WIDTH:]
        imag = both[:WIDTH, WIDTH:] - both[WIDTH:, :WIDTH]
        return real, imag

    def finish_first(chunk):
        columns = pl.ds(chunk * WIDTH, WIDTH)
        both = pl.ds(chunk * wide, wide)
        high, low = high_low(full0[chunk])
        m0_high[:, both] = high
        m0_low[:, both] = low
        lhs0[0, :, columns] = high[:, :WIDTH]
        lhs0[1, :, columns] = low[:, :WIDTH]
        lhs0[2, :, columns] = high[:, WIDTH:]
        lhs0[3, :, columns] = low[:, WIDTH:]

    def finish_second(chunk):
        both = pl.ds(chunk * wide, wide)
        high, low = high_low(full1[chunk].reshape(bands, wide))

        @pl.loop(0, chunks)
        def _(step):
            rows = pl.ds(pl.multiple_of(step * WIDTH, WIDTH), WIDTH)
            re_high, re_low = lhs0[0, rows], lhs0[1, rows]
            im_high, im_low = lhs0[2, rows], lhs0[3, rows]
            by_re = dot(re_high, high) + (dot(re_low, high) + dot(re_high, low))
            by_im = dot(im_high, high) + (dot(im_low, high) + dot(im_high, low))
            new_re = by_re[:, :WIDTH] - by_im[:, WIDTH:]
            new_im = by_re[:, WIDTH:] + by_im[:, :WIDTH]
            span_high, span_low = high_low(jnp.concatenate([new_re, new_im], 1))
            p_high[rows, both] = span_high
            p_low[rows, both] = span_low

    def scatter(part, at, plus, minus, arrived, pace):
        def add(where, buffer, which):
            part[where] = part[where] + buffer[which]

        far = up(reach)
        going_up = copy(part.at[at(far, 0)], plus.at[arrived(0, 0)], to_up)
        going_down = copy(part.at[at(far, 1)], minus.at[arrived(0, 1)], to_down)
        yield pace
        for step in range(1, reach):
            going_up.wait_recv()
            going_down.wait_recv()
            there_up, there_down = up(reach - step), down(reach - step)
            if step == 1:
                add(at(there_up, 0), plus, arrived(0, 0))
                add(at(there_down, 1), minus, arrived(0, 1))
            else:
                add(at(there_up), plus, arrived(step - 1))
                add(at(there_down), minus, arrived(step - 1))
            going_up = copy(part.at[at(there_up)], plus.at[arrived(step)], to_up)
            going_down = copy(part.at[at(there_down)], minus.at[arrived(step)], to_down)
            yield pace
        going_up.wait_recv()
        going_down.wait_recv()
        if reach == 1:
            add(at(z, 0), plus, arrived(0, 0))
            add(at(z, 1), minus, arrived(0, 1))
        else:
            here = at(z)
            part[here] = part[here] + plus[arrived(reach - 1)] + minus[arrived(reach - 1)]

    def gather(full, at, pace):
        from_core = []

        def send(target, *which):
            mine = full.at[at(*which)]
            return copy(mine, mine, target)

        for step in range(reach):
            if step:
                going_up.wait_recv()
                going_down.wait_recv()
            if step == reach - 1:
                going_up = send(to_up, down(step), 0)
                going_down = send(to_down, up(step), 1)
            else:
                going_up = send(to_up, down(step))
                going_down = send(to_down, up(step))
            from_core.append(send(to_core, down(step)))
            if step:
                from_core.append(send(to_core, up(step)))
            yield pace
        going_up.wait_recv()
        going_down.wait_recv()
        from_core.append(send(to_core, down(reach)))
        yield 1.2
        for crossing in from_core:
            crossing.wait_recv()

    def gather_in_two(full, at, pace):
        def send(target, *which):
            mine = full.at[at(*which)]
            return copy(mine, mine, target)

        two_up, two_down = send(to_up2, z), send(to_down2, z)
        one_up, one_down = send(to_up, z), send(to_down, z)
        from_core = [send(to_core, z)]
        yield pace
        two_up.wait_recv()
        later = [send(to_up2, down(2), 0), send(to_up, down(2))]
        two_down.wait_recv()
        later += [send(to_down2, up(2), 1), send(to_down, up(2))]
        from_core += [send(to_core, down(2)), send(to_core, up(2))]
        one_up.wait_recv()
        one_down.wait_recv()
        from_core += [send(to_core, down(1)), send(to_core, up(1))]
        yield pace
        later[1].wait_recv()
        later[3].wait_recv()
        from_core += [send(to_core, down(3)), send(to_core, up(3))]
        later[0].wait_recv()
        later[2].wait_recv()
        from_core.append(send(to_core, up(4)))
        yield 2.0
        for crossing in from_core:
            crossing.wait_recv()

    def first_margin(chunk):
        if chunk == 0:
            for load in loads:
                load.wait()

        @pl.loop(0, chunks)
        def _(block):
            rows = pl.ds(pl.multiple_of(block * WIDTH, WIDTH), WIDTH)
            real, imag = block_sum(st[0, block], st[1, chunk])
            part0[chunk, rows, :WIDTH] = real
            part0[chunk, rows, WIDTH:] = imag

        mine = pl.ds(pl.multiple_of(core * half, half), half)
        theirs = pl.ds(pl.multiple_of((1 - core) * half, half), half)
        crossing = copy(part0.at[chunk, theirs], core_in.at[chunk], to_core)
        yield 2.5
        crossing.wait_recv()
        part0[chunk, mine] = part0[chunk, mine] + core_in[chunk]

        def at(zz, h=None):
            count = piece if h is None else piece // 2
            start = core * half + zz * piece + (h or 0) * count
            return chunk, pl.ds(pl.multiple_of(start, 8), count)

        def arrived(step, h=None):
            count = piece if h is None else piece // 2
            return chunk, step, pl.ds((h or 0) * count, count)

        yield from scatter(part0, at, plus0, minus0, arrived, 3.2)
        crossing = copy(part0.at[at(z)], y_in.at[chunk], to_y)
        yield GATHER_START - (FIRST_START + 15.3)
        crossing.wait_recv()
        full0[at(z)] = part0[at(z)] + y_in[chunk]
        yield from gather(full0, at, 3.6)
        finish_first(chunk)

    def blocks_of(h):
        return pl.ds(0, chunks) if h is None else pl.ds(h * (chunks // 2), chunks // 2)

    def second_margin(chunk):
        for arriving in halo[chunk]:
            arriving.wait_recv()

        @pl.loop(0, chunks)
        def _(block):
            left_block = block * (1 - core) + chunk * core
            right_block = block * core + chunk * (1 - core)
            real, imag = block_sum(st[1 + core, left_block], st[2 - 2 * core, right_block])
            part1[chunk, block, :, :WIDTH] = real
            part1[chunk, block, :, WIDTH:] = imag

        def at(zz, h=None):
            return chunk, blocks_of(h), pl.ds(pl.multiple_of(zz * strip, 8), strip)

        def arrived(step, h=None):
            return chunk, step, blocks_of(h)

        yield from scatter(part1, at, plus1, minus1, arrived, SUM_PACE)

        def rows(c):
            return chunk, slice(None), pl.ds(pl.multiple_of(z * strip + c * thin, 8), thin)

        number = numbered[0]
        numbered[0] += 4
        ways = ((1 - core, 0), (core, 1), (1 - core, 1), (core, 0))
        from_zero = [
            prepare(part1.at[rows(c)], mix_columns.at[chunk, far], to_mix[n], number + n)
            for n, (c, far) in enumerate(ways[:3])
        ]
        from_one = [
            prepare(part1.at[rows(c)], mix_rows.at[chunk, far], to_mix[n], number + n)
            for n, (c, far) in enumerate(ways)
        ]
        joined.extend(from_zero)
        conditional.append(from_one[3])

        @pl.when(core == 0)
        def _():
            for made in from_zero:
                made.start()
            mix_columns[chunk, 0] = part1[rows(core)]

        @pl.when(core == 1)
        def _():
            for made in from_one:
                made.start()

        yield 4.5
        for made in from_zero:
            made.wait_recv()

        @pl.when(core == 1)
        def _():
            from_one[3].wait_recv()

    conditional = []
    joined = []

    def spread(chunk):
        def at(zz, h=None):
            return chunk, blocks_of(h), pl.ds(pl.multiple_of(zz * strip + core * thin, 8), thin)

        full1[at(z)] = (mix_columns[chunk, 0] + mix_columns[chunk, 1]) + (mix_rows[:, 0, chunk] + mix_rows[:, 1, chunk])
        if reach == 4 and chunk in IN_TWO:
            yield from gather_in_two(full1, at, FINAL_PACE)
        else:
            yield from gather(full1, at, 3.6)
        assert firsts == chunks
        finish_second(chunk)

    order = [(0.0, 0, "halo", states_across())]
    for chunk in range(chunks):
        order.append((FIRST_START + FIRST_PACE * chunk, len(order), "first", first_margin(chunk)))
    for chunk in range(chunks):
        order.append((HALO_START + HALO_PACE * chunk, len(order), "second", second_margin(chunk)))
    heapq.heapify(order)
    firsts = seconds = 0
    while order:
        when, n, kind, steps = heapq.heappop(order)
        wait = next(steps, None)
        if wait is not None:
            heapq.heappush(order, (when + wait, n, kind, steps))
        firsts += wait is None and kind == "first"
        seconds += wait is None and kind == "second"
        if wait is None and kind == "second" and seconds == chunks:
            for chunk in range(chunks):
                heapq.heappush(order, (when + SPREAD_PACE * chunk, 100 + chunk, "spread", spread(chunk)))

    def keep(h, value):
        high, low = high_low(value)
        stack[h] = jnp.concatenate([high[:, :half], low[:, :half], high[:, half:], low[:, half:]], 0)

    def product(high_ref, low_ref, h, chunk):
        deep, both = pl.ds(h * half, half), pl.ds(chunk * wide, wide)
        left = stack[h]
        short = jnp.concatenate([left[:own], left[2 * own:3 * own]], 0)
        with_high = dot(left, high_ref[deep, both])
        with_low = dot(short, low_ref[deep, both])
        by_re = with_high[:own] + (with_high[own:2 * own] + with_low[:own])
        by_im = with_high[2 * own:3 * own] + (with_high[3 * own:] + with_low[own:])
        return by_re[:, :WIDTH] - by_im[:, WIDTH:], by_re[:, WIDTH:] + by_im[:, :WIDTH]

    handed = [prepare(rows_out.at[h], rows_in.at[h], to_next) for h in range(2)]

    @pl.when(ka == 0)
    def _():
        for h in range(2):
            row = lax.broadcasted_iota(jnp.int32, (own, bands), 0) + pw * own
            column = lax.broadcasted_iota(jnp.int32, (own, bands), 1)
            keep(h, ((row == column + h * half) & (column < half)).astype(F32))

    @pl.when(ka > 0)
    def _():
        handed[0].wait_recv()
        keep(0, rows_in[0])

    begun = [product(p_high, p_low, 0, chunk) for chunk in range(chunks)]

    @pl.when(ka > 0)
    def _():
        handed[1].wait_recv()
        keep(1, rows_in[1])

    each = chunks // 2
    for h in range(2):
        for n in range(each):
            chunk = h * each + n
            more_re, more_im = product(p_high, p_low, 1, chunk)
            rows_out[h, :, pl.ds(n * WIDTH, WIDTH)] = begun[chunk][0] + more_re
            rows_out[h, :, pl.ds(half + n * WIDTH, WIDTH)] = begun[chunk][1] + more_im

        @pl.when(ka < ka_size - 1)
        def _():
            handed[h].start()

    for h in range(2):
        columns = pl.ds(h * half, half)
        out_ref[1, 0, :, columns] = rows_out[h, :, :half]
        out_ref[1, 1, :, columns] = rows_out[h, :, half:]
    for chunk in range(chunks):
        columns = pl.ds(chunk * WIDTH, WIDTH)
        first_re, first_im = product(m0_high, m0_low, 0, chunk)
        more_re, more_im = product(m0_high, m0_low, 1, chunk)
        out_ref[0, 0, :, columns] = first_re + more_re
        out_ref[0, 1, :, columns] = first_im + more_im

    for made in started + joined:
        made.wait_send()

    @pl.when(core == 1)
    def _():
        for made in conditional:
            made.wait_send()

    @pl.when(ka < ka_size - 1)
    def _():
        for made in handed:
            made.wait_send()


def shards(ka_size, pw_size, states_re, states_im):
    _, bands, waves = states_re.shape
    zsize = pw_size // 4
    own = bands // pw_size
    chunks = bands // WIDTH
    strip = WIDTH // zsize
    wide = 2 * WIDTH
    half = bands // 2
    piece = half // zsize
    reach = zsize // 2
    any_space = pl.BlockSpec(memory_space=pl.ANY)
    lines = pl.pallas_call(
        functools.partial(kernel, ka_size, zsize),
        out_shape=jax.ShapeDtypeStruct((2, 2, own, bands), F32),
        in_specs=[any_space, any_space],
        out_specs=pl.BlockSpec(memory_space=pltpu.VMEM),
        scratch_shapes=[
            pltpu.VMEM((3, chunks, 2, WIDTH, waves), BF16),
            pltpu.VMEM((chunks, bands, wide), F32),
            pltpu.VMEM((chunks, chunks, WIDTH, wide), F32),
            pltpu.VMEM((chunks, half, wide), F32),
            pltpu.VMEM((chunks, reach, piece, wide), F32),
            pltpu.VMEM((chunks, reach, piece, wide), F32),
            pltpu.VMEM((chunks, reach, chunks, strip, wide), F32),
            pltpu.VMEM((chunks, reach, chunks, strip, wide), F32),
            pltpu.VMEM((chunks, piece, wide), F32),
            pltpu.VMEM((chunks, 2, chunks, strip // 2, wide), F32),
            pltpu.VMEM((chunks, 2, chunks, strip // 2, wide), F32),
            pltpu.VMEM((chunks, bands, wide), F32),
            pltpu.VMEM((chunks, chunks, WIDTH, wide), F32),
            pltpu.VMEM((4, bands, bands), BF16),
            pltpu.VMEM((bands, 2 * bands), BF16),
            pltpu.VMEM((bands, 2 * bands), BF16),
            pltpu.VMEM((bands, 2 * bands), BF16),
            pltpu.VMEM((bands, 2 * bands), BF16),
            pltpu.VMEM((2, own, bands), F32),
            pltpu.VMEM((2, own, bands), F32),
            pltpu.VMEM((2, 4 * own, half), BF16),
            pltpu.SemaphoreType.DMA((4 * chunks,)),
            pltpu.SemaphoreType.DMA((SEMS,)),
            pltpu.SemaphoreType.DMA((SEMS,)),
        ],
        compiler_params=pltpu.CompilerParams(
            collective_id=0, has_side_effects=True, vmem_limit_bytes=56 * 1024 * 1024
        ),
    )(states_re, states_im)
    return jnp.transpose(lines, (0, 2, 1, 3))


def solution(mesh):
    in_specs = (P("ka", None, "pw"), P("ka", None, "pw"))
    out_specs = P("ka", "pw", None, None)
    body = functools.partial(shards, mesh.shape["ka"], mesh.shape["pw"])
    return jax.shard_map(body, mesh=mesh, in_specs=in_specs, out_specs=out_specs, check_vma=False)
```
